32 devices in a mesh: groups: 2 (over y), expert: 4 (over z), dp: 2 (over x), mp: 2 (over core).
Axes of the slice: x: 2, y: 2, z: 4, core: 2. Of those that a mesh axis runs over, the one named last changes fastest.
Arguments:
- hidden: bfloat16 [1024, 2048], P(('groups', 'expert', 'dp'), 'mp'), parts along dimension 0, may hold values from -6 to 6
- queries: bfloat16 [1024, 2048], P(('groups', 'expert', 'dp'), 'mp'), parts along dimension 0, may hold values from -6 to 120
- memory: bfloat16 [1024, 2, 2048], P(('groups', 'expert', 'dp'), None, 'mp'), parts along dimension 0, may hold values from -6 to 40.5
- target_pair: int32 [1024], P(('groups', 'expert', 'dp')), parts along dimension 0, may hold values from 0 to 15, as said below
- source_pair: int32 [1024], P(('groups', 'expert', 'dp')), parts along dimension 0, may hold values from 0 to 15, as said below
- routes: int32 [1024, 2], P(('groups', 'expert', 'dp')), parts along dimension 0, may hold values from 0 to 3, all different within a row; in each aligned block of 64 rows (0 to 63, 64 to 127, ...) at most 40 rows name the same one
- route_weight: float32 [1024, 2], P(('groups', 'expert', 'dp')), parts along dimension 0, may hold values from 0.1 to 1
- norm_gain: float32 [2048], replicated, may hold values from 0.5 to 1.5
- norm_bias: float32 [2048], replicated, may hold values from -3 to 3
- expert_in: bfloat16 [4, 2048, 8192], P('expert', None, ('dp', 'mp')), may hold values from -0.125 to 0.125
- expert_out: bfloat16 [4, 8192, 2048], P('expert', ('dp', 'mp')), may hold values from -0.0625 to 0.0625
Outputs:
- mixed: bfloat16 [1024, 2048], P(('groups', 'expert', 'dp'), 'mp'), parts along dimension 0
The draws below stay inside these ranges and needn't reach their ends.
There are 2 independent parts, one for each index of `groups`. The reference program is written for one: setup_inputs(seed, part) draws one part's arguments, and reference() takes and returns one part's arrays. A program takes and returns all parts, laid end to end along the dimension named above; an argument that names none is the same for every part. Nothing has to cross between parts.
Inputs may be any that keep to these rules, and one draw needn't show every extreme that they name: `target_pair`: within each batch pair numbers run over 0 to 15; each pair's target tokens form one contiguous run on one index of expert and dp, which holds the tokens of 4 pairs. `source_pair`: within each batch, memory rows read by expert index and then row carry pair numbers that never fall, and every pair has at least one row. `routes`: among the rows of one device no expert is named more than 40 times.
All inputs are finite; a program needn't handle non-finite values.
Results may differ from the reference program's by a relative error of at most 0.008.
Values may be sent and summed in bfloat16 or wider, within the bound.
A program may use at most 128 MiB of HBM per device.

```python
import math
import jax
import jax.numpy as jnp
import numpy as np
from jax import lax

D = 2048
HEADS = 16
HEAD = 128
FF = 8192
TOK_DEV = 64
SRC_DEV = 64
PAIRS_DEV = 4
EXPERTS = 4
BATCHES = 2
TOKENS = 512
SOURCE_ROWS = 512
PAIRS_ROW = 16
CAP = 40
N_DP = 2
N_MP = 2


def draw_queries(key, part):
    base = jnp.clip(jax.random.normal(key, (TOKENS, D), jnp.float32), -6.0, 6.0)
    return base.astype(jnp.bfloat16)


def draw_memory(key, part):
    base = jnp.clip(jax.random.normal(key, (SOURCE_ROWS, 2, D), jnp.float32), -6.0, 6.0)
    return base.astype(jnp.bfloat16)


def draw_source_pair(key, part):
    per_batch = SRC_DEV * EXPERTS

    def one_batch(subkey):
        cuts = jax.random.permutation(subkey, per_batch - 1)[:PAIRS_ROW - 1] + 1
        marks = jnp.zeros((per_batch,), jnp.int32).at[cuts].set(1)
        return jnp.cumsum(marks).astype(jnp.int32)
    pairs = jax.vmap(one_batch)(jax.random.split(key, BATCHES))
    pairs = pairs.reshape(BATCHES, EXPERTS, SRC_DEV)
    return jnp.swapaxes(pairs, 0, 1).reshape(SOURCE_ROWS).astype(jnp.int32)


def draw_target_pair(key, part):

    def one_batch(subkey):
        owner_key, cut_key = jax.random.split(subkey)
        owned = jax.random.permutation(owner_key, PAIRS_ROW).reshape(EXPERTS, PAIRS_DEV).astype(jnp.int32)

        def one_device(device_key, mine):
            cuts = jax.random.permutation(device_key, TOK_DEV - 1)[:PAIRS_DEV - 1] + 1
            marks = jnp.zeros((TOK_DEV,), jnp.int32).at[cuts].set(1)
            return mine[jnp.cumsum(marks)]
        return jax.vmap(one_device)(jax.random.split(cut_key, EXPERTS), owned)
    pairs = jax.vmap(one_batch)(jax.random.split(key, BATCHES))
    return jnp.swapaxes(pairs, 0, 1).reshape(TOKENS).astype(jnp.int32)


def levels(stream_key, extent, cuts, low, high):
    def one(axis_at, shards_of):
        heights = jax.random.uniform(jax.random.fold_in(jax.random.fold_in(stream_key, 6), axis_at), (shards_of,), jnp.float32, low / len(cuts), high / len(cuts))
        return jnp.repeat(jnp.exp(heights), extent[axis_at] // shards_of).reshape((-1,) + (1,) * (len(extent) - axis_at - 1))

    level = one(*cuts[0])
    for cut in cuts[1:]:
        level = level * one(*cut)
    return level


def routed_block(stream_key, own, number, rows, count, top, most, slope):
    sequence = jax.random.permutation(stream_key, count)
    packed, ordinary = portions_of(count, rows * top, most, slope, True), portions_of(count, rows * top, most, slope, False)
    places = jnp.arange(count)

    def named(tallies, rotation):
        used = int((tallies > 0).sum())
        fixed = max(1, used // 4)
        moved = fixed + (places - fixed + rotation * (used - fixed)) % max(1, count - fixed)
        return jnp.zeros((count,), jnp.int32).at[sequence[jnp.where(places < fixed, places, moved)]].set(jnp.asarray(tallies, jnp.int32))

    tallies = jnp.where(number % 4 == 0, named(packed, number // 4), named(ordinary, number - number // 4 - 1))
    mixed = jax.random.permutation(jax.random.fold_in(own, 3), count)
    donor, taker = mixed[0:count // 2 * 2:2], mixed[1:count // 2 * 2:2]
    margin = jnp.minimum(tallies[donor] - 1, most - tallies[taker]) // 2
    margin = jnp.where((donor == sequence[0]) | (taker == sequence[0]) | (tallies[taker] == 0), 0, jnp.maximum(margin, 0))
    moved = jax.random.randint(jax.random.fold_in(own, 4), (count // 2,), 0, 1 << 20) % (margin + 1)
    tallies = tallies.at[donor].add(-moved).at[taker].add(moved)
    items = jnp.searchsorted(jnp.cumsum(tallies), jnp.arange(rows * top), side="right").astype(jnp.int32)
    table = items.reshape(top, rows).T
    table = table[jax.random.permutation(jax.random.fold_in(own, 1), rows)]
    rotation = jax.random.randint(jax.random.fold_in(own, 2), (rows, 1), 0, top)
    return jnp.take_along_axis(table, (jnp.arange(top)[None, :] + rotation) % top, axis=1)


def portions_of(amount, total, bound, slope, full):
    portions = [(1 << 20) // math.isqrt(standing ** slope) + 1 for standing in range(1, amount + 1)]
    largest = bound if full else min(bound, max(-(-total // amount), total * portions[0] // sum(portions)))
    least = 1 if total - largest >= amount - 1 else 0
    holding, spare = [largest] + [least] * (amount - 1), total - largest - least * (amount - 1)
    while spare > 0:
        free = [i for i in range(1, amount) if holding[i] < largest] or [i for i in range(1, amount) if holding[i] < bound]
        whole, remaining = sum([portions[i] for i in free]), spare
        for i in free:
            addition = min(bound - holding[i], max(1, remaining * portions[i] // whole), spare)
            holding[i] = holding[i] + addition
            spare = spare - addition
    return np.array(holding)


def normal_values(rng, extent, width, most, cuts=(), kind=jnp.bfloat16):
    loudness = levels(rng, extent, cuts, -0.22, 0.18) if cuts else 1.0
    entries = jax.random.normal(rng, extent, jnp.float32) * width * loudness
    return jnp.minimum(jnp.maximum(entries, -most), most).astype(kind)


def setup_inputs(seed: int = 0, part: int = 0) -> dict:
    streams_of = jax.random.split(jax.random.key(seed), 12)
    part_splits = jax.random.split(jax.random.fold_in(streams_of[11], part), 12)
    hidden = normal_values(part_splits[0], (TOKENS, D), 1.0, 6.0, ((0, 8), (1, 2)))
    queries = draw_queries(jax.random.fold_in(jax.random.fold_in(streams_of[11], part), 71), part)
    memory = draw_memory(jax.random.fold_in(jax.random.fold_in(streams_of[11], part), 71), part)
    target_pair = draw_target_pair(jax.random.fold_in(jax.random.fold_in(streams_of[11], part), 71), part)
    source_pair = draw_source_pair(jax.random.fold_in(jax.random.fold_in(streams_of[11], part), 71), part)
    routes_keys = jax.random.split(jax.random.fold_in(part_splits[5], 1), TOKENS // TOK_DEV)
    routes_turns = jax.random.permutation(jax.random.fold_in(part_splits[5], 3), TOKENS // TOK_DEV)
    routes = jax.vmap(lambda own, number: routed_block(jax.random.fold_in(part_splits[5], 2), own, number, TOK_DEV, EXPERTS, 2, CAP, 2))(routes_keys, routes_turns).reshape((TOKENS, 2))
    route_weight = jnp.clip(0.1 + 0.9 * jax.random.uniform(part_splits[6], (TOKENS, 2), jnp.float32) ** levels(part_splits[6], (TOKENS, 2), ((0, 8),), -0.2, 0.2), 0.1, 1.0)
    norm_gain = jnp.clip(1.0 + 0.1 * jax.random.normal(streams_of[7], (D,), jnp.float32), 0.5, 1.5)
    norm_bias = normal_values(streams_of[8], (D,), 0.5, 3.0, (), jnp.float32)
    expert_in = normal_values(streams_of[9], (EXPERTS, D, FF), D ** -0.5, 0.125, ((0, 4), (2, 4)))
    expert_out = normal_values(streams_of[10], (EXPERTS, FF, D), FF ** -0.5, 0.0625, ((0, 4), (1, 4)))
    return {"hidden": hidden, "queries": queries, "memory": memory, "target_pair": target_pair, "source_pair": source_pair, "routes": routes, "route_weight": route_weight, "norm_gain": norm_gain, "norm_bias": norm_bias, "expert_in": expert_in, "expert_out": expert_out}


EPSILON = 1e-05
NEGATIVE = -1e+30

def rounded(values):
    return lax.optimization_barrier(values.astype(jnp.bfloat16)).astype(jnp.float32)

def layer_norm(rows, norm_gain, norm_bias):
    values = rows.astype(jnp.float32)
    center = lax.optimization_barrier(jnp.mean(values, axis=-1, keepdims=True))
    spread = lax.optimization_barrier(jnp.mean(jnp.square(values - center), axis=-1, keepdims=True))
    return rounded((values - center) * lax.rsqrt(spread + EPSILON) * norm_gain + norm_bias)

def by_batch(array, rows_dev):
    rest = array.shape[1:]
    shaped = array.reshape((EXPERTS, BATCHES, rows_dev) + rest)
    shaped = jnp.swapaxes(shaped, 0, 1)
    return shaped.reshape((BATCHES, EXPERTS * rows_dev) + rest)

def attend_batch(operands):
    query_rows, memory_rows, token_pairs, row_pairs = operands
    count = query_rows.shape[0]
    rows = memory_rows.shape[0]
    heads_q = query_rows.astype(jnp.float32).reshape(count, HEADS, HEAD)
    keys = memory_rows[:, 0, :].astype(jnp.float32).reshape(rows, HEADS, HEAD)
    values = memory_rows[:, 1, :].astype(jnp.float32).reshape(rows, HEADS, HEAD)
    score = jnp.einsum('thd,rhd->htr', heads_q, keys) * (1.0 / math.sqrt(HEAD))
    match = (token_pairs[:, None] == row_pairs[None, :])[None]
    masked = jnp.where(match, score, NEGATIVE)
    largest = lax.optimization_barrier(jnp.max(masked, axis=-1, keepdims=True))
    weight = jnp.where(match, jnp.exp(masked - largest), 0.0)
    total = lax.optimization_barrier(jnp.sum(weight, axis=-1))
    context = jnp.einsum('htr,rhd->thd', rounded(weight), values) / jnp.transpose(total)[:, :, None]
    return context.reshape(count, HEADS * HEAD)

def reference(hidden, queries, memory, target_pair, source_pair, routes, route_weight, norm_gain, norm_bias, expert_in, expert_out):
    context = lax.map(attend_batch, (by_batch(queries, TOK_DEV), by_batch(memory, SRC_DEV), by_batch(target_pair, TOK_DEV), by_batch(source_pair, SRC_DEV)))
    context = jnp.swapaxes(context.reshape(BATCHES, EXPERTS, TOK_DEV, D), 0, 1).reshape(TOKENS, D)
    attended = rounded(hidden.astype(jnp.float32) + context)
    sources = EXPERTS * BATCHES
    token_rows = attended.reshape(sources, TOK_DEV, D)
    flat = routes.reshape(sources, 2 * TOK_DEV)
    named = (flat[:, :, None] == jnp.arange(EXPERTS, dtype=jnp.int32)[None, None, :]).astype(jnp.int32)
    slot = lax.optimization_barrier(jnp.sum((jnp.cumsum(named, axis=1) - named) * named, axis=-1))
    dest = (flat * CAP + slot).astype(jnp.int32)
    place = (dest[:, :, None] == jnp.arange(EXPERTS * CAP, dtype=jnp.int32)[None, None, :]).astype(jnp.float32)
    per_token = lax.optimization_barrier(jnp.sum(place.reshape(sources, TOK_DEV, 2, EXPERTS * CAP), axis=2))
    sent = jnp.einsum('stk,std->skd', per_token, token_rows)
    by_expert = jnp.swapaxes(sent.reshape(sources, EXPERTS, CAP, D), 0, 1).reshape(EXPERTS, sources * CAP, D)
    slices = N_DP * N_MP

    def run_expert(operands):
        rows, weight_in, weight_out = operands
        normed = layer_norm(rows, norm_gain, norm_bias)
        w_first = weight_in.astype(jnp.float32).reshape(D, slices, FF // slices)
        w_second = weight_out.astype(jnp.float32).reshape(slices, FF // slices, D)
        active = rounded(jax.nn.relu(jnp.einsum('rd,dsf->srf', normed, w_first)))
        part = rounded(jnp.einsum('srf,sfc->src', active, w_second))
        return lax.optimization_barrier(jnp.sum(part, axis=0))
    outputs = lax.map(run_expert, (by_expert, expert_in, expert_out))
    by_source = jnp.swapaxes(outputs.reshape(EXPERTS, sources, CAP, D), 0, 1).reshape(sources, EXPERTS * CAP, D)
    picked = jax.vmap(lambda table, index: table[index])(by_source, dest)
    picked = picked.reshape(sources, TOK_DEV, 2, D)
    weights = route_weight.reshape(sources, TOK_DEV, 2)
    mixed = token_rows + lax.optimization_barrier(jnp.sum(weights[:, :, :, None] * picked, axis=2))
    return mixed.reshape(TOKENS, D).astype(jnp.bfloat16)
```

```python
import functools
import math

import jax
import jax.numpy as jnp
from jax import lax
from jax.experimental import pallas as pl
from jax.experimental.pallas import tpu as pltpu
from jax.sharding import PartitionSpec as P

HEAD = 128
EPSILON = 1e-05
NEGATIVE = -1e30
MESH = pl.DeviceIdType.MESH
F32 = jnp.float32
BF16 = jnp.bfloat16


def remote(src, dst, send, recv, **where):
    return pltpu.make_async_remote_copy(
        src_ref=src, dst_ref=dst, send_sem=send, recv_sem=recv, device_id=where, device_id_type=MESH
    )


def layer(
    E, DP, NC, NQ, C,
    kv_ref, sp_ref, q_ref, hid_ref, tp_ref, routes_ref, rw_ref, gain_ref, bias_ref, w1_hbm, w2_hbm,
    out_ref,
    kv, sp, w1, w2, att, stat_out, stat_in, sendbuf, xbuf, act, psend, pown, prec, xs, xr, zs, zr,
    wsem, lsem, kv_send, kv_recv, sp_send, sp_recv, st_send, st_recv,
    dz_send, dz_recv, dx_send, dx_recv, dp_send, dp_recv,
    rp_send, rp_recv, rx_send, rx_recv, rz_send, rz_recv,
):
    z = lax.axis_index("expert")
    x = lax.axis_index("dp")
    m = lax.axis_index("mp")
    T, W = q_ref.shape
    other = 1 - m
    S = sp_ref.shape[1]
    cols = W // NC
    wq = W // NQ
    FFL = w1.shape[1]
    EC = E * C

    copies_w = [
        pltpu.make_async_copy(w1_hbm, w1, wsem.at[0]),
        pltpu.make_async_copy(w2_hbm, w2, wsem.at[1]),
    ]
    own_kv = pltpu.make_async_copy(kv_ref, kv.at[z], lsem.at[0])
    own_kv.start()

    barrier = pltpu.get_barrier_semaphore()
    for d in range(1, E):
        pl.semaphore_signal(
            barrier, inc=1, device_id={"expert": lax.rem(z + d, E)}, device_id_type=MESH
        )
    for k in range(1, DP):
        pl.semaphore_signal(
            barrier, inc=1, device_id={"dp": lax.rem(x + k, DP)}, device_id_type=MESH
        )
    pl.semaphore_signal(barrier, inc=1, device_id={"mp": other}, device_id_type=MESH)
    pl.semaphore_wait(barrier, E - 1 + DP - 1 + 1)

    def hop(direction, h, c):
        owner = z - h if direction == 0 else z + h
        target = z + 1 if direction == 0 else z - 1
        src = kv_ref.at[c] if h == 0 else kv.at[owner, c]
        return remote(
            src, kv.at[owner, c], kv_send.at[direction, h, c], kv_recv.at[direction, h, c], expert=target
        )

    def sends(direction, h):
        if direction == 0:
            return jnp.logical_and(z >= h, z < E - 1)
        return jnp.logical_and(z <= E - 1 - h, z > 0)

    def arrived(direction, h, c):
        owner = z - h if direction == 0 else z + h
        return remote(
            kv.at[owner, c], kv.at[owner, c],
            kv_send.at[direction, h - 1, c], kv_recv.at[direction, h - 1, c], expert=owner,
        )

    for c in range(NC):
        for direction in range(2):
            @pl.when(sends(direction, 0))
            def _():
                hop(direction, 0, c).start()

    sp_copies = []
    for d in range(1, E):
        copy = remote(
            sp_ref, sp.at[z], sp_send.at[d - 1], sp_recv.at[d - 1], expert=lax.rem(z + d, E)
        )
        copy.start()
        sp_copies.append(copy)
    for copy in copies_w:
        copy.start()

    r0 = routes_ref[:, 0:1]
    r1 = routes_ref[:, 1:2]
    lane = lax.broadcasted_iota(jnp.int32, (T, 128), 1)
    member = jnp.logical_or(lane == r0, lane == r1).astype(F32).astype(BF16)
    tri = (
        lax.broadcasted_iota(jnp.int32, (T, T), 0) > lax.broadcasted_iota(jnp.int32, (T, T), 1)
    ).astype(F32).astype(BF16)
    slots = jnp.dot(tri, member, preferred_element_type=F32)
    slot0 = jnp.sum(jnp.where(lane == r0, slots, 0.0), axis=1, keepdims=True).astype(jnp.int32)
    slot1 = jnp.sum(jnp.where(lane == r1, slots, 0.0), axis=1, keepdims=True).astype(jnp.int32)
    place_lane = lax.broadcasted_iota(jnp.int32, (T, EC), 1)
    place0 = place_lane == r0 * C + slot0
    place1 = place_lane == r1 * C + slot1
    place = jnp.logical_or(place0, place1).astype(F32).astype(BF16)
    mixing = jnp.where(place0, rw_ref[:, 0:1], 0.0) + jnp.where(place1, rw_ref[:, 1:2], 0.0)
    mix_hi = mixing.astype(BF16)
    mix_lo = (mixing - mix_hi.astype(F32)).astype(BF16)

    for h in range(1, E):
        for c in range(NC):
            for direction in range(2):
                here = z >= h if direction == 0 else z <= E - 1 - h

                @pl.when(here)
                def _():
                    arrived(direction, h, c).wait_recv()

                if h < E - 1:
                    @pl.when(sends(direction, h))
                    def _():
                        hop(direction, h, c).start()
    own_kv.wait()
    for copy in sp_copies:
        copy.wait_recv()

    tp = tp_ref[...]
    match = jnp.concatenate(
        [jnp.where(j == z, sp_ref[...], sp[j]) for j in range(E)], axis=1
    ) == tp
    scale = 1.0 / math.sqrt(HEAD)
    for c in range(NC):
        for n in range(cols // HEAD):
            at = slice(n * HEAD, (n + 1) * HEAD)
            full = slice(c * cols + n * HEAD, c * cols + (n + 1) * HEAD)
            keys = kv[:, c, 0, :, at].reshape(E * S, HEAD)
            vals = kv[:, c, 1, :, at].reshape(E * S, HEAD)
            score = lax.dot_general(
                q_ref[:, full], keys, (((1,), (1,)), ((), ())), preferred_element_type=F32
            ) * scale
            masked = jnp.where(match, score, NEGATIVE)
            largest = jnp.max(masked, axis=1, keepdims=True)
            weight = jnp.where(match, jnp.exp(masked - largest), 0.0)
            total = jnp.sum(weight, axis=1, keepdims=True)
            context = jnp.dot(weight.astype(BF16), vals, preferred_element_type=F32) / total
            att[:, full] = (hid_ref[:, full].astype(F32) + context).astype(BF16)

    rows = att[...].astype(F32)
    mean = jnp.mean(rows, axis=1, keepdims=True)
    dev = rows - mean
    m2 = jnp.sum(dev * dev, axis=1, keepdims=True)
    stat_out[...] = jnp.where(lane == 0, mean, jnp.where(lane == 1, m2, 0.0))
    stat_copy = remote(stat_out, stat_in, st_send, st_recv, mp=other)
    stat_copy.start()
    stat_copy.wait_recv()
    mean_o = stat_in[:, 0:1]
    m2_o = stat_in[:, 1:2]
    center = (mean + mean_o) * 0.5
    gap = mean - mean_o
    var = (m2 + m2_o + gap * gap * (W * 0.5)) * (1.0 / (2 * W))
    normed = ((rows - center) * lax.rsqrt(var + EPSILON) * gain_ref[...] + bias_ref[...]).astype(BF16)
    outgoing = lax.dot_general(
        place, normed, (((0,), (0,)), ((), ())), preferred_element_type=F32
    ).astype(BF16)
    for e in range(E):
        sendbuf[e] = outgoing[e * C:(e + 1) * C]

    pending = []

    def spread(src, at, d):
        for k in range(1, DP):
            copy = remote(
                src, at, dx_send.at[k - 1, d], dx_recv.at[k - 1, d], dp=lax.rem(x + k, DP)
            )
            copy.start()
            pending.append(copy)
        copy = remote(src, at, dp_send.at[0, d], dp_recv.at[0, d], mp=other)
        copy.start()
        pending.append(copy)

    def block(half, xi, zi):
        return xbuf.at[half, xi * E + zi]

    for d in range(1, E):
        zd = lax.rem(z + d, E)
        copy = remote(
            sendbuf.at[zd], block(m, x, z), dz_send.at[d - 1], dz_recv.at[d - 1], expert=zd
        )
        copy.start()
        pending.append(copy)
    local = pltpu.make_async_copy(sendbuf.at[z], block(m, x, z), lsem.at[1])
    local.start()
    spread(sendbuf.at[z], block(m, x, z), 0)

    def landed(dst, recv):
        remote(dst, dst, st_send, recv, mp=other).wait_recv()

    for d in range(1, E):
        zs_from = lax.rem(z + E - d, E)
        mine = block(m, x, zs_from)
        landed(mine, dz_recv.at[d - 1])
        spread(mine, mine, d)
    local.wait()
    for d in range(E):
        landed(block(other, x, lax.rem(z + E - d, E)), dp_recv.at[0, d])

    copies_w[0].wait()

    TILE = 512

    def first(xi):
        left = xbuf[0, pl.ds(xi * E, E)].reshape(EC, W)
        right = xbuf[1, pl.ds(xi * E, E)].reshape(EC, W)
        rows_at = pl.ds(pl.multiple_of(xi * EC, 16), EC)

        def tile(j, carry):
            at = pl.ds(pl.multiple_of(j * TILE, TILE), TILE)
            hidden = jnp.dot(left, w1[0:W, at], preferred_element_type=F32)
            hidden = hidden + jnp.dot(right, w1[W:2 * W, at], preferred_element_type=F32)
            act[rows_at, at] = jnp.maximum(hidden, 0.0).astype(BF16)
            return carry

        lax.fori_loop(0, FFL // TILE, tile, 0)

    first(x)
    for k in range(1, DP):
        xi = lax.rem(x + DP - k, DP)
        for d in range(E):
            mine = block(m, xi, lax.rem(z + E - d, E))
            landed(mine, dx_recv.at[k - 1, d])
            copy = remote(mine, mine, dp_send.at[k, d], dp_recv.at[k, d], mp=other)
            copy.start()
            pending.append(copy)
        for d in range(E):
            landed(block(other, xi, lax.rem(z + E - d, E)), dp_recv.at[k, d])
        first(xi)

    copies_w[1].wait()
    R = DP * EC
    group = R if R <= 512 else EC

    def second(half, q, dst):
        at = pl.ds(pl.multiple_of(half * W + q * wq, wq), wq)

        def some(i, carry):
            rows_at = pl.ds(pl.multiple_of(i * group, 16), group)
            dst[q, rows_at, :] = jnp.dot(
                act[rows_at, :], w2[:, at], preferred_element_type=F32
            ).astype(BF16)
            return carry

        lax.fori_loop(0, R // group, some, 0)

    def column(xi):
        return pl.ds(pl.multiple_of(xi * EC, 16), EC)

    def reduce_mp(q):
        landed(prec.at[q], rp_recv.at[q])
        xs[q] = (pown[q].astype(F32) + prec[q].astype(F32)).astype(BF16)
        for k in range(1, DP):
            xd = lax.rem(x + k, DP)
            copy = remote(
                xs.at[q, column(xd)], xr.at[q, k - 1], rx_send.at[q, k - 1], rx_recv.at[q, k - 1], dp=xd
            )
            copy.start()
            pending.append(copy)

    for q in range(NQ):
        second(other, q, psend)
        copy = remote(psend.at[q], prec.at[q], rp_send.at[q], rp_recv.at[q], mp=other)
        copy.start()
        pending.append(copy)
        second(m, q, pown)
        if q >= 1:
            reduce_mp(q - 1)
    reduce_mp(NQ - 1)

    for q in range(NQ):
        total = xs[q, column(x), :].astype(F32)
        for k in range(1, DP):
            landed(xr.at[q, k - 1], rx_recv.at[q, k - 1])
            total = total + xr[q, k - 1].astype(F32)
        total = total.astype(BF16)
        for e in range(E):
            zs[q, e] = total[e * C:(e + 1) * C]
        for d in range(1, E):
            zd = lax.rem(z + d, E)
            copy = remote(
                zs.at[q, zd], zr.at[q, z], rz_send.at[q, d - 1], rz_recv.at[q, d - 1], expert=zd
            )
            copy.start()
            pending.append(copy)
        zr[q, pl.ds(z, 1)] = zs[q, pl.ds(z, 1)]

    for q in range(NQ):
        for d in range(1, E):
            landed(zr.at[q, lax.rem(z + E - d, E)], rz_recv.at[q, d - 1])
        back = zr[q].reshape(EC, wq)
        mixed = jnp.dot(mix_hi, back, preferred_element_type=F32)
        mixed = mixed + jnp.dot(mix_lo, back, preferred_element_type=F32)
        at = slice(q * wq, (q + 1) * wq)
        out_ref[:, at] = (att[:, at].astype(F32) + mixed).astype(BF16)

    for h in range(E - 1):
        for c in range(NC):
            for direction in range(2):
                @pl.when(sends(direction, h))
                def _():
                    hop(direction, h, c).wait_send()
    for copy in sp_copies:
        copy.wait_send()
    stat_copy.wait_send()
    for copy in pending:
        copy.wait_send()


def shards(
    hidden, queries, memory, target_pair, source_pair, routes, route_weight,
    norm_gain, norm_bias, expert_in, expert_out,
):
    E = lax.axis_size("expert")
    DP = lax.axis_size("dp")
    T, W = hidden.shape
    S = memory.shape[0]
    NC, NQ = 2, 4
    cap = 2 * T // E * 5 // 4
    C = -(-cap // 8) * 8
    cols, wq, EC = W // NC, W // NQ, E * C
    R = DP * EC
    FFL = expert_in.shape[2]
    kv = jnp.transpose(memory.reshape(S, 2, NC, cols), (2, 1, 0, 3))
    m = lax.axis_index("mp")
    gain = lax.dynamic_slice(norm_gain, (m * W,), (W,)).reshape(1, W)
    bias = lax.dynamic_slice(norm_bias, (m * W,), (W,)).reshape(1, W)
    vmem = pl.BlockSpec(memory_space=pltpu.VMEM)
    hbm = pl.BlockSpec(memory_space=pl.ANY)
    dma = pltpu.SemaphoreType.DMA
    return pl.pallas_call(
        functools.partial(layer, E, DP, NC, NQ, C),
        out_shape=jax.ShapeDtypeStruct((T, W), BF16),
        in_specs=[hbm] + [vmem] * 8 + [hbm] * 2,
        out_specs=vmem,
        scratch_shapes=[
            pltpu.VMEM((E, NC, 2, S, cols), BF16),
            pltpu.VMEM((E, 1, S), jnp.int32),
            pltpu.VMEM((2 * W, FFL), BF16),
            pltpu.VMEM((FFL, 2 * W), BF16),
            pltpu.VMEM((T, W), BF16),
            pltpu.VMEM((T, 128), F32),
            pltpu.VMEM((T, 128), F32),
            pltpu.VMEM((E, C, W), BF16),
            pltpu.VMEM((2, DP * E, C, W), BF16),
            pltpu.VMEM((R, FFL), BF16),
            pltpu.VMEM((NQ, R, wq), BF16),
            pltpu.VMEM((NQ, R, wq), BF16),
            pltpu.VMEM((NQ, R, wq), BF16),
            pltpu.VMEM((NQ, R, wq), BF16),
            pltpu.VMEM((NQ, max(DP - 1, 1), EC, wq), BF16),
            pltpu.VMEM((NQ, E, C, wq), BF16),
            pltpu.VMEM((NQ, E, C, wq), BF16),
            dma((2,)),
            dma((2,)),
            dma((2, E - 1, NC)),
            dma((2, E - 1, NC)),
            dma((E - 1,)),
            dma((E - 1,)),
            dma,
            dma,
            dma((E - 1,)),
            dma((E - 1,)),
            dma((DP - 1, E)),
            dma((DP - 1, E)),
            dma((DP, E)),
            dma((DP, E)),
            dma((NQ,)),
            dma((NQ,)),
            dma((NQ, DP - 1)),
            dma((NQ, DP - 1)),
            dma((NQ, E - 1)),
            dma((NQ, E - 1)),
        ],
        compiler_params=pltpu.CompilerParams(
            collective_id=0, has_side_effects=True, vmem_limit_bytes=60 * 1024 * 1024
        ),
    )(
        kv, source_pair.reshape(1, S), queries, hidden, target_pair.reshape(T, 1), routes, route_weight,
        gain, bias,
        expert_in.reshape(2 * W, FFL), expert_out.reshape(FFL, 2 * W),
    )


def solution(mesh):
    rows = ("groups", "expert", "dp")
    return jax.shard_map(
        shards,
        mesh=mesh,
        in_specs=(
            P(rows, "mp"),
            P(rows, "mp"),
            P(rows, None, "mp"),
            P(rows),
            P(rows),
            P(rows, None),
            P(rows, None),
            P(),
            P(),
            P("expert", None, ("dp", "mp")),
            P("expert", ("dp", "mp"), None),
        ),
        out_specs=P(rows, "mp"),
        check_vma=False,
    )
```

```python
import functools
import math

import jax
import jax.numpy as jnp
from jax import lax
from jax.experimental import pallas as pl
from jax.experimental.pallas import tpu as pltpu
from jax.sharding import PartitionSpec as P

HEAD = 128
EPSILON = 1e-05
NEGATIVE = -1e30
MESH = pl.DeviceIdType.MESH
F32 = jnp.float32
BF16 = jnp.bfloat16


def remote(src, dst, send, recv, **where):
    return pltpu.make_async_remote_copy(
        src_ref=src, dst_ref=dst, send_sem=send, recv_sem=recv, device_id=where, device_id_type=MESH
    )


def layer(
    E, DP, NC, NQ, C,
    kv_ref, sp_ref, q_ref, hid_ref, tp_ref, routes_ref, rw_ref, gain_ref, bias_ref, w1_hbm, w2_hbm,
    out_ref,
    q_end, tp_end, num_out, num_in, aux_out, aux_in, near_num, end_send, end_recv, pt_send, pt_recv,
    kv, sp, w1, w2, att, stat_out, stat_in, sendbuf, xbuf, act, psend, pown, prec, xs, xr, zs, zr,
    wsem, lsem, kv_send, kv_recv, sp_send, sp_recv, st_send, st_recv,
    dz_send, dz_recv, dx_send, dx_recv, dp_send, dp_recv,
    rp_send, rp_recv, rx_send, rx_recv, rz_send, rz_recv,
):
    z = lax.axis_index("expert")
    x = lax.axis_index("dp")
    m = lax.axis_index("mp")
    T, W = q_ref.shape
    other = 1 - m
    S = sp_ref.shape[1]
    cols = W // NC
    wq = W // NQ
    FFL = w1.shape[1]
    EC = E * C

    copies_w = [
        pltpu.make_async_copy(w1_hbm, w1, wsem.at[0]),
        pltpu.make_async_copy(w2_hbm, w2, wsem.at[1]),
    ]
    own_kv = pltpu.make_async_copy(kv_ref, kv.at[z], lsem.at[0])
    own_kv.start()

    barrier = pltpu.get_barrier_semaphore()
    for d in range(1, E):
        pl.semaphore_signal(
            barrier, inc=1, device_id={"expert": lax.rem(z + d, E)}, device_id_type=MESH
        )
    for k in range(1, DP):
        pl.semaphore_signal(
            barrier, inc=1, device_id={"dp": lax.rem(x + k, DP)}, device_id_type=MESH
        )
    pl.semaphore_signal(barrier, inc=1, device_id={"mp": other}, device_id_type=MESH)
    pl.semaphore_wait(barrier, E - 1 + DP - 1 + 1)

    def hop(direction, h, c):
        owner = z - h if direction == 0 else z + h
        target = z + 1 if direction == 0 else z - 1
        src = kv_ref.at[c] if h == 0 else kv.at[owner, c]
        return remote(
            src, kv.at[owner, c], kv_send.at[direction, h, c], kv_recv.at[direction, h, c], expert=target
        )

    def sends(direction, h):
        if direction == 0:
            ok = jnp.logical_and(z >= h, z < E - 1)
            return ok if h == 0 else jnp.logical_and(ok, z < E - 2)
        ok = jnp.logical_and(z <= E - 1 - h, z > 0)
        return ok if h == 0 else jnp.logical_and(ok, z > 1)

    def comes(direction, h):
        if direction == 0:
            ok = z >= h
            return ok if h == 1 else jnp.logical_and(ok, z < E - 1)
        ok = z <= E - 1 - h
        return ok if h == 1 else jnp.logical_and(ok, z > 0)

    is_end = jnp.logical_or(z == 0, z == E - 1)
    is_helper = jnp.logical_or(z == 1, z == E - 2)
    end = jnp.where(z == 1, 0, E - 1)
    helper = jnp.where(z == 0, 1, E - 2)
    q_copy = remote(q_ref, q_end, end_send.at[0], end_recv.at[0], expert=helper)
    tp_copy = remote(tp_ref, tp_end, end_send.at[1], end_recv.at[1], expert=helper)

    def part_copies(c):
        return [
            remote(num_out.at[c], num_in.at[c], pt_send.at[0, c], pt_recv.at[0, c], expert=end),
            remote(aux_out.at[c], aux_in.at[c], pt_send.at[1, c], pt_recv.at[1, c], expert=end),
        ]

    def arrived(direction, h, c):
        owner = z - h if direction == 0 else z + h
        return remote(
            kv.at[owner, c], kv.at[owner, c],
            kv_send.at[direction, h - 1, c], kv_recv.at[direction, h - 1, c], expert=owner,
        )

    sp_copies = []
    for d in range(1, E):
        copy = remote(
            sp_ref, sp.at[z], sp_send.at[d - 1], sp_recv.at[d - 1], expert=lax.rem(z + d, E)
        )
        copy.start()
        sp_copies.append(copy)
    @pl.when(is_end)
    def _():
        tp_copy.start()

    for c in range(NC):
        for direction in range(2):
            @pl.when(sends(direction, 0))
            def _():
                hop(direction, 0, c).start()

    @pl.when(is_end)
    def _():
        q_copy.start()

    for copy in copies_w:
        copy.start()

    eye = lax.broadcasted_iota(jnp.int32, (T, T), 0) == lax.broadcasted_iota(jnp.int32, (T, T), 1)

    def upright(row):
        return jnp.sum(jnp.where(eye, row.astype(F32), 0.0), axis=1, keepdims=True)

    r0 = upright(routes_ref[0:1, :]).astype(jnp.int32)
    r1 = upright(routes_ref[1:2, :]).astype(jnp.int32)
    lane = lax.broadcasted_iota(jnp.int32, (T, 128), 1)
    member = jnp.logical_or(lane == r0, lane == r1).astype(F32).astype(BF16)
    tri = (
        lax.broadcasted_iota(jnp.int32, (T, T), 0) > lax.broadcasted_iota(jnp.int32, (T, T), 1)
    ).astype(F32).astype(BF16)
    slots = jnp.dot(tri, member, preferred_element_type=F32)
    slot0 = jnp.sum(jnp.where(lane == r0, slots, 0.0), axis=1, keepdims=True).astype(jnp.int32)
    slot1 = jnp.sum(jnp.where(lane == r1, slots, 0.0), axis=1, keepdims=True).astype(jnp.int32)
    place_lane = lax.broadcasted_iota(jnp.int32, (T, EC), 1)
    place0 = place_lane == r0 * C + slot0
    place1 = place_lane == r1 * C + slot1
    place = jnp.logical_or(place0, place1).astype(F32).astype(BF16)
    mixing = jnp.where(place0, upright(rw_ref[0:1, :]), 0.0)
    mixing = mixing + jnp.where(place1, upright(rw_ref[1:2, :]), 0.0)
    mix_hi = mixing.astype(BF16)
    mix_lo = (mixing - mix_hi.astype(F32)).astype(BF16)

    tp = upright(tp_ref[...]).astype(jnp.int32)
    own_kv.wait()
    for copy in sp_copies:
        copy.wait_recv()
    pairs = [jnp.where(j == z, sp_ref[...], sp[j]) for j in range(E)]
    all_pairs = jnp.concatenate(pairs, axis=1)
    scale = 1.0 / math.sqrt(HEAD)

    def attend(query, keys, vals, match):
        score = lax.dot_general(
            query, keys, (((1,), (1,)), ((), ())), preferred_element_type=F32
        ) * scale
        masked = jnp.where(match, score, NEGATIVE)
        largest = jnp.max(masked, axis=1, keepdims=True)
        weight = jnp.where(match, jnp.exp(masked - largest), 0.0)
        total = jnp.sum(weight, axis=1, keepdims=True)
        return largest, total, jnp.dot(weight.astype(BF16), vals, preferred_element_type=F32)

    def heads(c):
        for n in range(cols // HEAD):
            yield n, slice(n * HEAD, (n + 1) * HEAD), slice(c * cols + n * HEAD, c * cols + (n + 1) * HEAD)

    def flat(column):
        return jnp.sum(jnp.where(eye, column, 0.0), axis=0, keepdims=True)

    def help_end(c):
        tpe = upright(tp_end[...]).astype(jnp.int32)
        far = jnp.concatenate(
            [jnp.where(jnp.logical_or(j == z, j == end), -1, pairs[j]) for j in range(E)], axis=1
        )
        match = far == tpe
        for n, at, full in heads(c):
            keys = kv[:, c, 0, :, at].reshape(E * S, HEAD)
            vals = kv[:, c, 1, :, at].reshape(E * S, HEAD)
            largest, total, num = attend(q_end[:, full], keys, vals, match)
            num_out[c, :, at] = num.astype(BF16)
            aux_out[c, 2 * n:2 * n + 1, :] = flat(largest)
            aux_out[c, 2 * n + 1:2 * n + 2, :] = flat(total)
        for copy in part_copies(c):
            copy.start()

    for h in range(1, E - 1):
        if h == E - 2:
            @pl.when(is_helper)
            def _():
                q_copy.wait_recv()
                tp_copy.wait_recv()

        for c in range(NC):
            for direction in range(2):
                @pl.when(comes(direction, h))
                def _():
                    arrived(direction, h, c).wait_recv()

                if h < E - 2:
                    @pl.when(sends(direction, h))
                    def _():
                        hop(direction, h, c).start()

            if h == E - 2:
                @pl.when(is_helper)
                def _():
                    help_end(c)

    @pl.when(jnp.logical_not(is_end))
    def _():
        match = all_pairs == tp
        for c in range(NC):
            for n, at, full in heads(c):
                keys = kv[:, c, 0, :, at].reshape(E * S, HEAD)
                vals = kv[:, c, 1, :, at].reshape(E * S, HEAD)
                _, total, num = attend(q_ref[:, full], keys, vals, match)
                att[:, full] = (hid_ref[:, full].astype(F32) + num / total).astype(BF16)

    @pl.when(is_end)
    def _():
        near = jnp.concatenate(
            [sp_ref[...], jnp.where(z == 0, pairs[1], pairs[E - 2])], axis=1
        )
        match = near == tp
        mine = []
        for c in range(NC):
            for n, at, full in heads(c):
                keys = jnp.concatenate([kv[z, c, 0, :, at], kv[helper, c, 0, :, at]], axis=0)
                vals = jnp.concatenate([kv[z, c, 1, :, at], kv[helper, c, 1, :, at]], axis=0)
                largest, total, num = attend(q_ref[:, full], keys, vals, match)
                near_num[:, full] = num
                mine.append((largest, total))
        for c in range(NC):
            for copy in part_copies(c):
                copy.wait_recv()
            for n, at, full in heads(c):
                largest, total = mine[c * (cols // HEAD) + n]
                largest_far = upright(aux_in[c, 2 * n:2 * n + 1, :])
                total_far = upright(aux_in[c, 2 * n + 1:2 * n + 2, :])
                top = jnp.maximum(largest, largest_far)
                near_scale = jnp.exp(largest - top)
                far_scale = jnp.exp(largest_far - top)
                num = near_num[:, full] * near_scale + num_in[c, :, at].astype(F32) * far_scale
                context = num / (total * near_scale + total_far * far_scale)
                att[:, full] = (hid_ref[:, full].astype(F32) + context).astype(BF16)

    rows = att[...].astype(F32)
    mean = jnp.mean(rows, axis=1, keepdims=True)
    dev = rows - mean
    m2 = jnp.sum(dev * dev, axis=1, keepdims=True)
    stat_out[...] = jnp.where(lane == 0, mean, jnp.where(lane == 1, m2, 0.0))
    stat_copy = remote(stat_out, stat_in, st_send, st_recv, mp=other)
    stat_copy.start()
    stat_copy.wait_recv()
    mean_o = stat_in[:, 0:1]
    m2_o = stat_in[:, 1:2]
    center = (mean + mean_o) * 0.5
    gap = mean - mean_o
    var = (m2 + m2_o + gap * gap * (W * 0.5)) * (1.0 / (2 * W))
    half_at = pl.ds(pl.multiple_of(m * W, 128), W)
    gain = gain_ref[:, half_at]
    bias = bias_ref[:, half_at]
    normed = ((rows - center) * lax.rsqrt(var + EPSILON) * gain + bias).astype(BF16)
    outgoing = lax.dot_general(
        place, normed, (((0,), (0,)), ((), ())), preferred_element_type=F32
    ).astype(BF16)
    for e in range(E):
        sendbuf[e] = outgoing[e * C:(e + 1) * C]

    pending = []

    def spread(src, at, d):
        for k in range(1, DP):
            copy = remote(
                src, at, dx_send.at[k - 1, d], dx_recv.at[k - 1, d], dp=lax.rem(x + k, DP)
            )
            copy.start()
            pending.append(copy)
        copy = remote(src, at, dp_send.at[0, d], dp_recv.at[0, d], mp=other)
        copy.start()
        pending.append(copy)

    def block(half, xi, zi):
        return xbuf.at[half, xi * E + zi]

    for d in range(1, E):
        zd = lax.rem(z + d, E)
        copy = remote(
            sendbuf.at[zd], block(m, x, z), dz_send.at[d - 1], dz_recv.at[d - 1], expert=zd
        )
        copy.start()
        pending.append(copy)
    local = pltpu.make_async_copy(sendbuf.at[z], block(m, x, z), lsem.at[1])
    local.start()
    spread(sendbuf.at[z], block(m, x, z), 0)

    def landed(dst, recv):
        remote(dst, dst, st_send, recv, mp=other).wait_recv()

    for d in range(1, E):
        zs_from = lax.rem(z + E - d, E)
        mine = block(m, x, zs_from)
        landed(mine, dz_recv.at[d - 1])
        spread(mine, mine, d)
    local.wait()
    for d in range(E):
        landed(block(other, x, lax.rem(z + E - d, E)), dp_recv.at[0, d])

    copies_w[0].wait()

    TILE = 512

    def first(xi):
        left = xbuf[0, pl.ds(xi * E, E)].reshape(EC, W)
        right = xbuf[1, pl.ds(xi * E, E)].reshape(EC, W)
        rows_at = pl.ds(pl.multiple_of(xi * EC, 16), EC)

        def tile(j, carry):
            at = pl.ds(pl.multiple_of(j * TILE, TILE), TILE)
            hidden = jnp.dot(left, w1[0:W, at], preferred_element_type=F32)
            hidden = hidden + jnp.dot(right, w1[W:2 * W, at], preferred_element_type=F32)
            act[rows_at, at] = jnp.maximum(hidden, 0.0).astype(BF16)
            return carry

        lax.fori_loop(0, FFL // TILE, tile, 0)

    first(x)
    for k in range(1, DP):
        xi = lax.rem(x + DP - k, DP)
        for d in range(E):
            mine = block(m, xi, lax.rem(z + E - d, E))
            landed(mine, dx_recv.at[k - 1, d])
            copy = remote(mine, mine, dp_send.at[k, d], dp_recv.at[k, d], mp=other)
            copy.start()
            pending.append(copy)
        for d in range(E):
            landed(block(other, xi, lax.rem(z + E - d, E)), dp_recv.at[k, d])
        first(xi)

    copies_w[1].wait()
    def column(xi):
        return pl.ds(pl.multiple_of(xi * EC, 16), EC)

    def second(half, q, xi, dst):
        at = pl.ds(pl.multiple_of(half * W + q * wq, wq), wq)
        dst[q, column(xi), :] = jnp.dot(
            act[column(xi), :], w2[:, at], preferred_element_type=F32
        ).astype(BF16)

    def swap(q, k):
        xi = lax.rem(x + k, DP)
        second(other, q, xi, psend)
        copy = remote(
            psend.at[q, column(xi)], prec.at[q, column(xi)],
            rp_send.at[q, k], rp_recv.at[q, k], mp=other,
        )
        copy.start()
        pending.append(copy)
        second(m, q, xi, pown)

    def both(q, k):
        xi = lax.rem(x + k, DP)
        landed(prec.at[q, column(xi)], rp_recv.at[q, k])
        return pown[q, column(xi), :].astype(F32) + prec[q, column(xi), :].astype(F32)

    def pass_on(q):
        for k in range(1, DP):
            xd = lax.rem(x + k, DP)
            xs[q, column(xd), :] = both(q, k).astype(BF16)
            copy = remote(
                xs.at[q, column(xd)], xr.at[q, k - 1], rx_send.at[q, k - 1], rx_recv.at[q, k - 1], dp=xd
            )
            copy.start()
            pending.append(copy)

    for q in range(NQ):
        for k in range(1, DP):
            swap(q, k)
        if q >= 1:
            pass_on(q - 1)
    pass_on(NQ - 1)

    for q in range(NQ):
        swap(q, 0)

    for q in range(NQ):
        total = both(q, 0)
        for k in range(1, DP):
            landed(xr.at[q, k - 1], rx_recv.at[q, k - 1])
            total = total + xr[q, k - 1].astype(F32)
        total = total.astype(BF16)
        for e in range(E):
            zs[q, e] = total[e * C:(e + 1) * C]
        for d in range(1, E):
            zd = lax.rem(z + d, E)
            copy = remote(
                zs.at[q, zd], zr.at[q, z], rz_send.at[q, d - 1], rz_recv.at[q, d - 1], expert=zd
            )
            copy.start()
            pending.append(copy)
        zr[q, pl.ds(z, 1)] = zs[q, pl.ds(z, 1)]

    for q in range(NQ):
        for d in range(1, E):
            landed(zr.at[q, lax.rem(z + E - d, E)], rz_recv.at[q, d - 1])
        back = zr[q].reshape(EC, wq)
        mixed = jnp.dot(mix_hi, back, preferred_element_type=F32)
        mixed = mixed + jnp.dot(mix_lo, back, preferred_element_type=F32)
        at = slice(q * wq, (q + 1) * wq)
        out_ref[:, at] = (att[:, at].astype(F32) + mixed).astype(BF16)

    for h in range(E - 1):
        for c in range(NC):
            for direction in range(2):
                @pl.when(sends(direction, h))
                def _():
                    hop(direction, h, c).wait_send()
    @pl.when(is_end)
    def _():
        q_copy.wait_send()
        tp_copy.wait_send()

    @pl.when(is_helper)
    def _():
        for c in range(NC):
            for copy in part_copies(c):
                copy.wait_send()

    for copy in sp_copies:
        copy.wait_send()
    stat_copy.wait_send()
    for copy in pending:
        copy.wait_send()


def shards(
    hidden, queries, memory, target_pair, source_pair, routes, route_weight,
    norm_gain, norm_bias, expert_in, expert_out,
):
    E = lax.axis_size("expert")
    DP = lax.axis_size("dp")
    T, W = hidden.shape
    S = memory.shape[0]
    NC, NQ = 4, 4
    cap = 2 * T // E * 5 // 4
    C = -(-cap // 8) * 8
    cols, wq, EC = W // NC, W // NQ, E * C
    R = DP * EC
    FFL = expert_in.shape[2]
    kv = jnp.transpose(memory.reshape(S, 2, NC, cols), (2, 1, 0, 3))
    vmem = pl.BlockSpec(memory_space=pltpu.VMEM)
    hbm = pl.BlockSpec(memory_space=pl.ANY)
    dma = pltpu.SemaphoreType.DMA
    return pl.pallas_call(
        functools.partial(layer, E, DP, NC, NQ, C),
        out_shape=jax.ShapeDtypeStruct((T, W), BF16),
        in_specs=[hbm] + [vmem] * 8 + [hbm] * 2,
        out_specs=vmem,
        scratch_shapes=[
            pltpu.VMEM((T, W), BF16),
            pltpu.VMEM((1, T), jnp.int32),
            pltpu.VMEM((NC, T, cols), BF16),
            pltpu.VMEM((NC, T, cols), BF16),
            pltpu.VMEM((NC, 8, T), F32),
            pltpu.VMEM((NC, 8, T), F32),
            pltpu.VMEM((T, W), F32),
            dma((2,)),
            dma((2,)),
            dma((2, NC)),
            dma((2, NC)),
            pltpu.VMEM((E, NC, 2, S, cols), BF16),
            pltpu.VMEM((E, 1, S), jnp.int32),
            pltpu.VMEM((2 * W, FFL), BF16),
            pltpu.VMEM((FFL, 2 * W), BF16),
            pltpu.VMEM((T, W), BF16),
            pltpu.VMEM((T, 128), F32),
            pltpu.VMEM((T, 128), F32),
            pltpu.VMEM((E, C, W), BF16),
            pltpu.VMEM((2, DP * E, C, W), BF16),
            pltpu.VMEM((R, FFL), BF16),
            pltpu.VMEM((NQ, R, wq), BF16),
            pltpu.VMEM((NQ, R, wq), BF16),
            pltpu.VMEM((NQ, R, wq), BF16),
            pltpu.VMEM((NQ, R, wq), BF16),
            pltpu.VMEM((NQ, max(DP - 1, 1), EC, wq), BF16),
            pltpu.VMEM((NQ, E, C, wq), BF16),
            pltpu.VMEM((NQ, E, C, wq), BF16),
            dma((2,)),
            dma((2,)),
            dma((2, E - 1, NC)),
            dma((2, E - 1, NC)),
            dma((E - 1,)),
            dma((E - 1,)),
            dma,
            dma,
            dma((E - 1,)),
            dma((E - 1,)),
            dma((DP - 1, E)),
            dma((DP - 1, E)),
            dma((DP, E)),
            dma((DP, E)),
            dma((NQ, DP)),
            dma((NQ, DP)),
            dma((NQ, DP - 1)),
            dma((NQ, DP - 1)),
            dma((NQ, E - 1)),
            dma((NQ, E - 1)),
        ],
        compiler_params=pltpu.CompilerParams(
            collective_id=0, has_side_effects=True, vmem_limit_bytes=60 * 1024 * 1024
        ),
    )(
        kv, source_pair.reshape(1, S), queries, hidden, target_pair.reshape(1, T), routes.T, route_weight.T,
        norm_gain.reshape(1, 2 * W), norm_bias.reshape(1, 2 * W),
        expert_in.reshape(2 * W, FFL), expert_out.reshape(FFL, 2 * W),
    )


def solution(mesh):
    rows = ("groups", "expert", "dp")
    return jax.shard_map(
        shards,
        mesh=mesh,
        in_specs=(
            P(rows, "mp"),
            P(rows, "mp"),
            P(rows, None, "mp"),
            P(rows),
            P(rows),
            P(rows, None),
            P(rows, None),
            P(),
            P(),
            P("expert", None, ("dp", "mp")),
            P("expert", ("dp", "mp"), None),
        ),
        out_specs=P(rows, "mp"),
        check_vma=False,
    )
```

```python
import functools
import math

import jax
import jax.numpy as jnp
from jax import lax
from jax.experimental import pallas as pl
from jax.experimental.pallas import tpu as pltpu
from jax.sharding import PartitionSpec as P

HEAD = 128
EPSILON = 1e-05
NEGATIVE = -1e30
MESH = pl.DeviceIdType.MESH
F32 = jnp.float32
BF16 = jnp.bfloat16


def remote(src, dst, send, recv, **where):
    return pltpu.make_async_remote_copy(
        src_ref=src, dst_ref=dst, send_sem=send, recv_sem=recv, device_id=where, device_id_type=MESH
    )


def layer(
    E, DP, NC, NQ, C,
    kv_ref, sp_ref, q_hbm, hid_hbm, tp_ref, routes_ref, rw_ref, gain_ref, bias_ref, w1_hbm, w2_hbm,
    out_ref,
    q_ref, hid_ref, q_end, tp_end, num_out, num_in, aux_out, aux_in, near_num, end_send, end_recv, pt_send, pt_recv, own_sem,
    kv, sp, w1, w2, att, stat_out, stat_in, sendbuf, xbuf, act, psend, pown, prec, xs, xr, zs, zr,
    wsem, lsem, kv_send, kv_recv, sp_send, sp_recv, st_send, st_recv,
    dz_send, dz_recv, dx_send, dx_recv, dp_send, dp_recv,
    rp_send, rp_recv, rx_send, rx_recv, rz_send, rz_recv,
):
    z = lax.axis_index("expert")
    x = lax.axis_index("dp")
    m = lax.axis_index("mp")
    T, W = q_ref.shape
    other = 1 - m
    S = sp_ref.shape[1]
    cols = W // NC
    wq = W // NQ
    FFL = w1.shape[1]
    EC = E * C

    copies_w = [
        pltpu.make_async_copy(w1_hbm, w1, wsem.at[0]),
        pltpu.make_async_copy(w2_hbm, w2, wsem.at[1]),
    ]
    def own_block(c):
        return kv_ref.at[:, :, pl.ds(c * cols, cols)]

    own_kv = [pltpu.make_async_copy(own_block(c), kv.at[z, c], own_sem.at[c]) for c in range(NC)]
    for copy in own_kv:
        copy.start()
    q_in = pltpu.make_async_copy(q_hbm, q_ref, lsem.at[0])
    hid_in = pltpu.make_async_copy(hid_hbm, hid_ref, wsem.at[2])
    q_in.start()
    hid_in.start()

    barrier = pltpu.get_barrier_semaphore()
    for d in range(1, E):
        pl.semaphore_signal(
            barrier, inc=1, device_id={"expert": lax.rem(z + d, E)}, device_id_type=MESH
        )
    for k in range(1, DP):
        pl.semaphore_signal(
            barrier, inc=1, device_id={"dp": lax.rem(x + k, DP)}, device_id_type=MESH
        )
    pl.semaphore_signal(barrier, inc=1, device_id={"mp": other}, device_id_type=MESH)
    pl.semaphore_wait(barrier, E - 1 + DP - 1 + 1)

    def hop(direction, h, c):
        owner = z - h if direction == 0 else z + h
        target = z + 1 if direction == 0 else z - 1
        src = own_block(c) if h == 0 else kv.at[owner, c]
        return remote(
            src, kv.at[owner, c], kv_send.at[direction, h, c], kv_recv.at[direction, h, c], expert=target
        )

    def sends(direction, h):
        if direction == 0:
            ok = jnp.logical_and(z >= h, z < E - 1)
            return ok if h == 0 else jnp.logical_and(ok, z < E - 2)
        ok = jnp.logical_and(z <= E - 1 - h, z > 0)
        return ok if h == 0 else jnp.logical_and(ok, z > 1)

    def comes(direction, h):
        if direction == 0:
            ok = z >= h
            return ok if h == 1 else jnp.logical_and(ok, z < E - 1)
        ok = z <= E - 1 - h
        return ok if h == 1 else jnp.logical_and(ok, z > 0)

    is_end = jnp.logical_or(z == 0, z == E - 1)
    is_helper = jnp.logical_or(z == 1, z == E - 2)
    end = jnp.where(z == 1, 0, E - 1)
    helper = jnp.where(z == 0, 1, E - 2)
    q_copy = remote(q_hbm, q_end, end_send.at[0], end_recv.at[0], expert=helper)
    tp_copy = remote(tp_ref, tp_end, end_send.at[1], end_recv.at[1], expert=helper)

    def part_copies(c):
        return [
            remote(num_out.at[c], num_in.at[c], pt_send.at[0, c], pt_recv.at[0, c], expert=end),
            remote(aux_out.at[c], aux_in.at[c], pt_send.at[1, c], pt_recv.at[1, c], expert=end),
        ]

    def arrived(direction, h, c):
        owner = z - h if direction == 0 else z + h
        return remote(
            kv.at[owner, c], kv.at[owner, c],
            kv_send.at[direction, h - 1, c], kv_recv.at[direction, h - 1, c], expert=owner,
        )

    sp_copies = []
    for d in range(1, E):
        copy = remote(
            sp_ref, sp.at[z], sp_send.at[d - 1], sp_recv.at[d - 1], expert=lax.rem(z + d, E)
        )
        copy.start()
        sp_copies.append(copy)
    @pl.when(is_end)
    def _():
        tp_copy.start()

    for c in range(NC):
        for direction in range(2):
            @pl.when(sends(direction, 0))
            def _():
                hop(direction, 0, c).start()

    @pl.when(is_end)
    def _():
        q_copy.start()

    for copy in copies_w:
        copy.start()

    eye = lax.broadcasted_iota(jnp.int32, (T, T), 0) == lax.broadcasted_iota(jnp.int32, (T, T), 1)

    def upright(row):
        return jnp.sum(jnp.where(eye, row.astype(F32), 0.0), axis=1, keepdims=True)

    r0 = upright(routes_ref[0:1, :]).astype(jnp.int32)
    r1 = upright(routes_ref[1:2, :]).astype(jnp.int32)
    lane = lax.broadcasted_iota(jnp.int32, (T, 128), 1)
    member = jnp.logical_or(lane == r0, lane == r1).astype(F32).astype(BF16)
    tri = (
        lax.broadcasted_iota(jnp.int32, (T, T), 0) > lax.broadcasted_iota(jnp.int32, (T, T), 1)
    ).astype(F32).astype(BF16)
    slots = jnp.dot(tri, member, preferred_element_type=F32)
    slot0 = jnp.sum(jnp.where(lane == r0, slots, 0.0), axis=1, keepdims=True).astype(jnp.int32)
    slot1 = jnp.sum(jnp.where(lane == r1, slots, 0.0), axis=1, keepdims=True).astype(jnp.int32)
    place_lane = lax.broadcasted_iota(jnp.int32, (T, EC), 1)
    place0 = place_lane == r0 * C + slot0
    place1 = place_lane == r1 * C + slot1
    place = jnp.logical_or(place0, place1).astype(F32).astype(BF16)
    mixing = jnp.where(place0, upright(rw_ref[0:1, :]), 0.0)
    mixing = mixing + jnp.where(place1, upright(rw_ref[1:2, :]), 0.0)
    mix_hi = mixing.astype(BF16)
    mix_lo = (mixing - mix_hi.astype(F32)).astype(BF16)

    tp = upright(tp_ref[...]).astype(jnp.int32)
    for copy in own_kv:
        copy.wait()
    q_in.wait()
    hid_in.wait()
    for copy in sp_copies:
        copy.wait_recv()
    pairs = [jnp.where(j == z, sp_ref[...], sp[j]) for j in range(E)]
    all_pairs = jnp.concatenate(pairs, axis=1)
    scale = 1.0 / math.sqrt(HEAD)

    def attend(query, keys, vals, match):
        score = lax.dot_general(
            query, keys, (((1,), (1,)), ((), ())), preferred_element_type=F32
        ) * scale
        masked = jnp.where(match, score, NEGATIVE)
        largest = jnp.max(masked, axis=1, keepdims=True)
        weight = jnp.where(match, jnp.exp(masked - largest), 0.0)
        total = jnp.sum(weight, axis=1, keepdims=True)
        return largest, total, jnp.dot(weight.astype(BF16), vals, preferred_element_type=F32)

    def heads(c):
        for n in range(cols // HEAD):
            yield n, slice(n * HEAD, (n + 1) * HEAD), slice(c * cols + n * HEAD, c * cols + (n + 1) * HEAD)

    def flat(column):
        return jnp.sum(jnp.where(eye, column, 0.0), axis=0, keepdims=True)

    def help_end(c):
        tpe = upright(tp_end[...]).astype(jnp.int32)
        far = jnp.concatenate(
            [jnp.where(jnp.logical_or(j == z, j == end), -1, pairs[j]) for j in range(E)], axis=1
        )
        match = far == tpe
        for n, at, full in heads(c):
            keys = kv[:, c, 0, :, at].reshape(E * S, HEAD)
            vals = kv[:, c, 1, :, at].reshape(E * S, HEAD)
            largest, total, num = attend(q_end[:, full], keys, vals, match)
            num_out[c, :, at] = num.astype(BF16)
            aux_out[c, 2 * n:2 * n + 1, :] = flat(largest)
            aux_out[c, 2 * n + 1:2 * n + 2, :] = flat(total)
        for copy in part_copies(c):
            copy.start()

    for h in range(1, E - 1):
        if h == E - 2:
            @pl.when(is_helper)
            def _():
                q_copy.wait_recv()
                tp_copy.wait_recv()

        for c in range(NC):
            for direction in range(2):
                @pl.when(comes(direction, h))
                def _():
                    arrived(direction, h, c).wait_recv()

                if h < E - 2:
                    @pl.when(sends(direction, h))
                    def _():
                        hop(direction, h, c).start()

            if h == E - 2:
                @pl.when(is_helper)
                def _():
                    help_end(c)

    @pl.when(jnp.logical_not(is_end))
    def _():
        match = all_pairs == tp
        for c in range(NC):
            for n, at, full in heads(c):
                keys = kv[:, c, 0, :, at].reshape(E * S, HEAD)
                vals = kv[:, c, 1, :, at].reshape(E * S, HEAD)
                _, total, num = attend(q_ref[:, full], keys, vals, match)
                att[:, full] = (hid_ref[:, full].astype(F32) + num / total).astype(BF16)

    @pl.when(is_end)
    def _():
        near = jnp.concatenate(
            [sp_ref[...], jnp.where(z == 0, pairs[1], pairs[E - 2])], axis=1
        )
        match = near == tp
        mine = []
        for c in range(NC):
            for n, at, full in heads(c):
                keys = jnp.concatenate([kv[z, c, 0, :, at], kv[helper, c, 0, :, at]], axis=0)
                vals = jnp.concatenate([kv[z, c, 1, :, at], kv[helper, c, 1, :, at]], axis=0)
                largest, total, num = attend(q_ref[:, full], keys, vals, match)
                near_num[:, full] = num
                mine.append((largest, total))
        for c in range(NC):
            for copy in part_copies(c):
                copy.wait_recv()
            for n, at, full in heads(c):
                largest, total = mine[c * (cols // HEAD) + n]
                largest_far = upright(aux_in[c, 2 * n:2 * n + 1, :])
                total_far = upright(aux_in[c, 2 * n + 1:2 * n + 2, :])
                top = jnp.maximum(largest, largest_far)
                near_scale = jnp.exp(largest - top)
                far_scale = jnp.exp(largest_far - top)
                num = near_num[:, full] * near_scale + num_in[c, :, at].astype(F32) * far_scale
                context = num / (total * near_scale + total_far * far_scale)
                att[:, full] = (hid_ref[:, full].astype(F32) + context).astype(BF16)

    rows = att[...].astype(F32)
    mean = jnp.mean(rows, axis=1, keepdims=True)
    dev = rows - mean
    m2 = jnp.sum(dev * dev, axis=1, keepdims=True)
    stat_out[...] = jnp.where(lane == 0, mean, jnp.where(lane == 1, m2, 0.0))
    stat_copy = remote(stat_out, stat_in, st_send, st_recv, mp=other)
    stat_copy.start()
    stat_copy.wait_recv()
    mean_o = stat_in[:, 0:1]
    m2_o = stat_in[:, 1:2]
    center = (mean + mean_o) * 0.5
    gap = mean - mean_o
    var = (m2 + m2_o + gap * gap * (W * 0.5)) * (1.0 / (2 * W))
    half_at = pl.ds(pl.multiple_of(m * W, 128), W)
    gain = gain_ref[:, half_at]
    bias = bias_ref[:, half_at]
    normed = ((rows - center) * lax.rsqrt(var + EPSILON) * gain + bias).astype(BF16)
    outgoing = lax.dot_general(
        place, normed, (((0,), (0,)), ((), ())), preferred_element_type=F32
    ).astype(BF16)
    for e in range(E):
        sendbuf[e] = outgoing[e * C:(e + 1) * C]

    pending = []

    def spread(src, at, d):
        for k in range(1, DP):
            copy = remote(
                src, at, dx_send.at[k - 1, d], dx_recv.at[k - 1, d], dp=lax.rem(x + k, DP)
            )
            copy.start()
            pending.append(copy)
        copy = remote(src, at, dp_send.at[0, d], dp_recv.at[0, d], mp=other)
        copy.start()
        pending.append(copy)

    def block(half, xi, zi):
        return xbuf.at[half, xi * E + zi]

    for d in range(1, E):
        zd = lax.rem(z + d, E)
        copy = remote(
            sendbuf.at[zd], block(m, x, z), dz_send.at[d - 1], dz_recv.at[d - 1], expert=zd
        )
        copy.start()
        pending.append(copy)
    local = pltpu.make_async_copy(sendbuf.at[z], block(m, x, z), lsem.at[1])
    local.start()
    spread(sendbuf.at[z], block(m, x, z), 0)

    def landed(dst, recv):
        remote(dst, dst, st_send, recv, mp=other).wait_recv()

    for d in range(1, E):
        zs_from = lax.rem(z + E - d, E)
        mine = block(m, x, zs_from)
        landed(mine, dz_recv.at[d - 1])
        spread(mine, mine, d)
    local.wait()
    for d in range(E):
        landed(block(other, x, lax.rem(z + E - d, E)), dp_recv.at[0, d])

    copies_w[0].wait()

    TILE = 512

    def first(xi):
        left = xbuf[0, pl.ds(xi * E, E)].reshape(EC, W)
        right = xbuf[1, pl.ds(xi * E, E)].reshape(EC, W)
        rows_at = pl.ds(pl.multiple_of(xi * EC, 16), EC)

        def tile(j, carry):
            at = pl.ds(pl.multiple_of(j * TILE, TILE), TILE)
            hidden = jnp.dot(left, w1[0:W, at], preferred_element_type=F32)
            hidden = hidden + jnp.dot(right, w1[W:2 * W, at], preferred_element_type=F32)
            act[rows_at, at] = jnp.maximum(hidden, 0.0).astype(BF16)
            return carry

        lax.fori_loop(0, FFL // TILE, tile, 0)

    first(x)
    for k in range(1, DP):
        xi = lax.rem(x + DP - k, DP)
        for d in range(E):
            mine = block(m, xi, lax.rem(z + E - d, E))
            landed(mine, dx_recv.at[k - 1, d])
            copy = remote(mine, mine, dp_send.at[k, d], dp_recv.at[k, d], mp=other)
            copy.start()
            pending.append(copy)
        for d in range(E):
            landed(block(other, xi, lax.rem(z + E - d, E)), dp_recv.at[k, d])
        first(xi)

    copies_w[1].wait()
    def column(xi):
        return pl.ds(pl.multiple_of(xi * EC, 16), EC)

    def second(half, q, xi, dst):
        at = pl.ds(pl.multiple_of(half * W + q * wq, wq), wq)
        dst[q, column(xi), :] = jnp.dot(
            act[column(xi), :], w2[:, at], preferred_element_type=F32
        ).astype(BF16)

    def swap(q, k):
        xi = lax.rem(x + k, DP)
        second(other, q, xi, psend)
        copy = remote(
            psend.at[q, column(xi)], prec.at[q, column(xi)],
            rp_send.at[q, k], rp_recv.at[q, k], mp=other,
        )
        copy.start()
        pending.append(copy)
        second(m, q, xi, pown)

    def both(q, k):
        xi = lax.rem(x + k, DP)
        landed(prec.at[q, column(xi)], rp_recv.at[q, k])
        return pown[q, column(xi), :].astype(F32) + prec[q, column(xi), :].astype(F32)

    def pass_on(q):
        for k in range(1, DP):
            xd = lax.rem(x + k, DP)
            xs[q, column(xd), :] = both(q, k).astype(BF16)
            copy = remote(
                xs.at[q, column(xd)], xr.at[q, k - 1], rx_send.at[q, k - 1], rx_recv.at[q, k - 1], dp=xd
            )
            copy.start()
            pending.append(copy)

    for q in range(NQ):
        for k in range(1, DP):
            swap(q, k)
        if q >= 1:
            pass_on(q - 1)
    pass_on(NQ - 1)

    for q in range(NQ):
        swap(q, 0)

    for q in range(NQ):
        total = both(q, 0)
        for k in range(1, DP):
            landed(xr.at[q, k - 1], rx_recv.at[q, k - 1])
            total = total + xr[q, k - 1].astype(F32)
        total = total.astype(BF16)
        for e in range(E):
            zs[q, e] = total[e * C:(e + 1) * C]
        for d in range(1, E):
            zd = lax.rem(z + d, E)
            copy = remote(
                zs.at[q, zd], zr.at[q, z], rz_send.at[q, d - 1], rz_recv.at[q, d - 1], expert=zd
            )
            copy.start()
            pending.append(copy)
        zr[q, pl.ds(z, 1)] = zs[q, pl.ds(z, 1)]

    for q in range(NQ):
        for d in range(1, E):
            landed(zr.at[q, lax.rem(z + E - d, E)], rz_recv.at[q, d - 1])
        back = zr[q].reshape(EC, wq)
        mixed = jnp.dot(mix_hi, back, preferred_element_type=F32)
        mixed = mixed + jnp.dot(mix_lo, back, preferred_element_type=F32)
        at = slice(q * wq, (q + 1) * wq)
        out_ref[:, at] = (att[:, at].astype(F32) + mixed).astype(BF16)

    for h in range(E - 1):
        for c in range(NC):
            for direction in range(2):
                @pl.when(sends(direction, h))
                def _():
                    hop(direction, h, c).wait_send()
    @pl.when(is_end)
    def _():
        q_copy.wait_send()
        tp_copy.wait_send()

    @pl.when(is_helper)
    def _():
        for c in range(NC):
            for copy in part_copies(c):
                copy.wait_send()

    for copy in sp_copies:
        copy.wait_send()
    stat_copy.wait_send()
    for copy in pending:
        copy.wait_send()


def shards(
    hidden, queries, memory, target_pair, source_pair, routes, route_weight,
    norm_gain, norm_bias, expert_in, expert_out,
):
    E = lax.axis_size("expert")
    DP = lax.axis_size("dp")
    T, W = hidden.shape
    S = memory.shape[0]
    NC, NQ = 4, 4
    cap = 2 * T // E * 5 // 4
    C = -(-cap // 8) * 8
    cols, wq, EC = W // NC, W // NQ, E * C
    R = DP * EC
    FFL = expert_in.shape[2]
    kv = jnp.transpose(memory, (1, 0, 2))
    vmem = pl.BlockSpec(memory_space=pltpu.VMEM)
    hbm = pl.BlockSpec(memory_space=pl.ANY)
    dma = pltpu.SemaphoreType.DMA
    return pl.pallas_call(
        functools.partial(layer, E, DP, NC, NQ, C),
        out_shape=jax.ShapeDtypeStruct((T, W), BF16),
        in_specs=[hbm, vmem, hbm, hbm] + [vmem] * 5 + [hbm] * 2,
        out_specs=vmem,
        scratch_shapes=[
            pltpu.VMEM((T, W), BF16),
            pltpu.VMEM((T, W), BF16),
            pltpu.VMEM((T, W), BF16),
            pltpu.VMEM((1, T), jnp.int32),
            pltpu.VMEM((NC, T, cols), BF16),
            pltpu.VMEM((NC, T, cols), BF16),
            pltpu.VMEM((NC, 8, T), F32),
            pltpu.VMEM((NC, 8, T), F32),
            pltpu.VMEM((T, W), F32),
            dma((2,)),
            dma((2,)),
            dma((2, NC)),
            dma((2, NC)),
            dma((NC,)),
            pltpu.VMEM((E, NC, 2, S, cols), BF16),
            pltpu.VMEM((E, 1, S), jnp.int32),
            pltpu.VMEM((2 * W, FFL), BF16),
            pltpu.VMEM((FFL, 2 * W), BF16),
            pltpu.VMEM((T, W), BF16),
            pltpu.VMEM((T, 128), F32),
            pltpu.VMEM((T, 128), F32),
            pltpu.VMEM((E, C, W), BF16),
            pltpu.VMEM((2, DP * E, C, W), BF16),
            pltpu.VMEM((R, FFL), BF16),
            pltpu.VMEM((NQ, R, wq), BF16),
            pltpu.VMEM((NQ, R, wq), BF16),
            pltpu.VMEM((NQ, R, wq), BF16),
            pltpu.VMEM((NQ, R, wq), BF16),
            pltpu.VMEM((NQ, max(DP - 1, 1), EC, wq), BF16),
            pltpu.VMEM((NQ, E, C, wq), BF16),
            pltpu.VMEM((NQ, E, C, wq), BF16),
            dma((3,)),
            dma((2,)),
            dma((2, E - 1, NC)),
            dma((2, E - 1, NC)),
            dma((E - 1,)),
            dma((E - 1,)),
            dma,
            dma,
            dma((E - 1,)),
            dma((E - 1,)),
            dma((DP - 1, E)),
            dma((DP - 1, E)),
            dma((DP, E)),
            dma((DP, E)),
            dma((NQ, DP)),
            dma((NQ, DP)),
            dma((NQ, DP - 1)),
            dma((NQ, DP - 1)),
            dma((NQ, E - 1)),
            dma((NQ, E - 1)),
        ],
        compiler_params=pltpu.CompilerParams(
            collective_id=0, has_side_effects=True, vmem_limit_bytes=60 * 1024 * 1024
        ),
    )(
        kv, source_pair.reshape(1, S), queries, hidden, target_pair.reshape(1, T), routes.T, route_weight.T,
        norm_gain.reshape(1, 2 * W), norm_bias.reshape(1, 2 * W),
        expert_in.reshape(2 * W, FFL), expert_out.reshape(FFL, 2 * W),
    )


def solution(mesh):
    rows = ("groups", "expert", "dp")
    return jax.shard_map(
        shards,
        mesh=mesh,
        in_specs=(
            P(rows, "mp"),
            P(rows, "mp"),
            P(rows, None, "mp"),
            P(rows),
            P(rows),
            P(rows, None),
            P(rows, None),
            P(),
            P(),
            P("expert", None, ("dp", "mp")),
            P("expert", ("dp", "mp"), None),
        ),
        out_specs=P(rows, "mp"),
        check_vma=False,
    )
```
